512 devices in a mesh: pair: 64 (over z, x, core), cuts: 8 (over y).
Axes of the slice: x: 4, y: 8, z: 8, core: 2. Of those that a mesh axis runs over, the one named last changes fastest.
Arguments:
- amplitudes: bfloat16 [65536, 2048], P('pair'), may hold values from -6 to 6
- factors: bfloat16 [128, 24, 128, 128], P('pair', 'cuts'), may hold values from -0.5 to 0.5
- screening: int32 [32, 16], replicated, may hold values from 0 to 127, as said below
- tile_slot: int32 [128], replicated, may hold values from 0 to 127, as said below
- pair_orbitals: int32 [32, 2], replicated, may hold values from 0 to 3999
- occupied_energy: float32 [4000], replicated, may hold values from -2 to -0.3
- virtual_energy: float32 [128, 128], replicated, may hold values from 0.2 to 3
Outputs:
- scaled_residual: float32 [65536, 2048], P(('pair', 'cuts'))
The draws below stay inside these ranges and needn't reach their ends.
Inputs may be any that keep to these rules, and one draw needn't show every extreme that they name: `screening`: call tile_slot[t] // 2 the owner of tile t. The 16 tiles named by one pair have 16 different owners. `tile_slot`: every tile has its own slot.
All inputs are finite; a program needn't handle non-finite values.
Results may differ from the reference program's by a relative error of at most 0.012.
Values may be sent and summed in bfloat16 or wider, within the bound.
A program may use at most 64 MiB of HBM per device.

```python
import jax
import jax.numpy as jnp
from jax import lax

TILE = 128
TILE_DEV = 2
K = 16
NQ_CUT = 3
NOCC = 4000
PAIRS = 32
NTILE = 128
NQ = 24
N_CUTS = 8


def shared_layout(key):
    owner_count = NTILE // TILE_DEV
    slot_of_tile = jax.random.permutation(jax.random.fold_in(key, 7), NTILE).astype(jnp.int32)
    tile_of_slot = jnp.argsort(slot_of_tile, stable=True).astype(jnp.int32)
    weights = 2 ** jax.random.randint(jax.random.fold_in(key, 11), (owner_count,), 0, 4)
    raw_scores = jax.random.randint(jax.random.fold_in(key, 13), (PAIRS, owner_count), 0, 65536)
    scores = raw_scores * weights[None, :] * owner_count + jnp.arange(owner_count, dtype=jnp.int32)[None, :]
    top_values, chosen_owners = lax.top_k(scores, K)
    local_index = jax.random.randint(jax.random.fold_in(key, 17), chosen_owners.shape, 0, TILE_DEV)
    slots = chosen_owners.astype(jnp.int32) * TILE_DEV + local_index
    tiles = tile_of_slot[slots]
    return (slot_of_tile, tiles.reshape(PAIRS, K).astype(jnp.int32))


def draw_screening(key, part):
    return shared_layout(key)[1]


def draw_tile_slot(key, part):
    return shared_layout(key)[0]


def plant(array, own_key, low, high):
    spot = [jax.random.randint(jax.random.fold_in(own_key, axis), (), 0, length) for axis, length in enumerate(array.shape)]
    longest = array.shape.index(max(array.shape))
    next_to = spot[:longest] + [(spot[longest] + 1) % array.shape[longest]] + spot[longest + 1:]
    return array.at[tuple(spot)].set(low).at[tuple(next_to)].set(high)


def block_scale(own_key, extent, shards, smallest, high):
    level, own = 1.0, jax.random.fold_in(own_key, 6)
    for position, shards_of in shards:
        draws = jnp.exp(jax.random.uniform(jax.random.fold_in(own, position), (shards_of,), jnp.float32, smallest / len(shards), high / len(shards)))
        level = level * jnp.repeat(draws, extent[position] // shards_of).reshape([-1 if axis == position else 1 for axis in range(len(extent))])
    return level


def noise(stream_key, extent, scale, limit, split=(), kind=jnp.bfloat16):
    values = scale * jax.random.normal(stream_key, extent, jnp.float32)
    if split:
        values = values * block_scale(stream_key, extent, split, -0.22, 0.18)
    return jnp.clip(values, -limit, limit).astype(kind)


def setup_inputs(seed: int = 0) -> dict:
    key_list = jax.random.split(jax.random.key(seed), 8)
    amplitudes = noise(key_list[0], (PAIRS * K * TILE, K * TILE), 1.0, 6.0, ((0, 64),))
    factors = noise(key_list[1], (NTILE, NQ, TILE, TILE), TILE ** -0.5, 0.5, ((0, 64), (1, 8)))
    screening = draw_screening(jax.random.fold_in(key_list[7], 71), 0)
    tile_slot = draw_tile_slot(jax.random.fold_in(key_list[7], 71), 0)
    pair_orbitals = plant(jax.random.randint(key_list[4], (PAIRS, 2), 0, NOCC), jax.random.fold_in(key_list[4], 1), 0, NOCC - 1).astype(jnp.int32)
    occupied_energy = jnp.clip(jax.random.uniform(key_list[5], (NOCC,), jnp.float32, -2.0, -0.3), -2.0, -0.3)
    virtual_energy = jnp.clip(jax.random.uniform(key_list[6], (NTILE, TILE), jnp.float32, 0.2, 3.0), 0.2, 3.0)
    return dict(amplitudes=amplitudes, factors=factors, screening=screening, tile_slot=tile_slot, pair_orbitals=pair_orbitals, occupied_energy=occupied_energy, virtual_energy=virtual_energy)


def reference(amplitudes, factors, screening, tile_slot, pair_orbitals, occupied_energy, virtual_energy):
    def one_pair(inputs):
        block_rows, tiles, orbitals = inputs
        slots = tile_slot[tiles]
        chosen = factors[slots].astype(jnp.float32)
        blocks = block_rows.astype(jnp.float32).reshape(K, TILE, K * TILE)
        ladder = jnp.zeros((K * TILE, K * TILE), jnp.float32)
        for cut_index in range(N_CUTS):
            running = jnp.zeros((K, TILE, K, TILE), jnp.float32)
            for vector in range(NQ_CUT):
                factor_left = chosen[:, cut_index * NQ_CUT + vector]
                half_done = jnp.einsum("iac,icx->iax", factor_left, blocks)
                half_done = lax.optimization_barrier(half_done.astype(jnp.bfloat16)).astype(jnp.float32)
                running = running + jnp.einsum("iajd,jbd->iajb", half_done.reshape(K, TILE, K, TILE), factor_left)
            rounded = lax.optimization_barrier(running.reshape(K * TILE, K * TILE).astype(jnp.bfloat16))
            ladder = ladder + rounded.astype(jnp.float32)
        tile_energy = virtual_energy[tiles].reshape(K * TILE)
        row_energy = tile_energy - occupied_energy[orbitals[0]]
        col_energy = tile_energy - occupied_energy[orbitals[1]]
        return ladder / (row_energy[:, None] + col_energy[None, :])

    stacked = amplitudes.reshape(PAIRS, K * TILE, K * TILE)
    result = lax.map(one_pair, (stacked, screening, pair_orbitals))
    return result.reshape(PAIRS * K * TILE, K * TILE)
```

```python
import jax
import jax.numpy as jnp
from jax import lax
from jax.experimental import pallas as pl
from jax.experimental.pallas import tpu as pltpu
from jax.sharding import PartitionSpec as P

TILE = 128
K = 16
NQ = 3
NZ, NX, NC, NY = 8, 4, 2, 8
NS = NX * NC
SL = TILE // NS
SLOTS = 128
BLOCK = SLOTS // NZ
ROWS = 8
SUBS = 4
SJ = K // SUBS
BF16 = jnp.bfloat16
F32 = jnp.float32
MESH = pl.DeviceIdType.MESH

GATHER_ORDER = sorted(
    [(q, t) for q in range(NQ) for t in range(1, 5)], key=lambda a: a[1] + 1.5 * a[0]
)


def ladder_kernel(
    amp, fac, screen, slot_of, orb, occ, virt, out,
    a_buf, gath0, gath1, gath2, sel, tiles, half, part, snd, rcv, rec,
    a_sem, loc_sem, sp_s, sp_r, ag_s, ag_r, dl_s, dl_r, ex_s, ex_r, rs_s, rs_r,
):
    gath = (gath0, gath1, gath2)
    pair = lax.axis_index("pair")
    y = lax.axis_index("cuts")
    s = lax.rem(pair, NS)
    z = pair // NS
    x = s // NC
    core = lax.rem(s, NC)
    p = pair // NC

    def wrap(value, n):
        return lax.rem(value + n, n)

    z_up, z_down = wrap(z + 1, NZ) * NS + s, wrap(z - 1, NZ) * NS + s
    y_up, y_down = wrap(y + 1, NY), wrap(y - 1, NY)

    load_a = pltpu.make_async_copy(amp, a_buf, a_sem)
    load_a.start()

    barrier = pltpu.get_barrier_semaphore()
    peers = [(z * NS + wrap(s + d, NS), y) for d in range(1, NS)]
    peers += [(z_up, y), (z_down, y), (pair, y_up), (pair, y_down)]
    for peer in peers:
        pl.semaphore_signal(barrier, inc=1, device_id=peer, device_id_type=MESH)
    pl.semaphore_wait(barrier, len(peers))

    def remote(src, dst, send, recv, device):
        copy = pltpu.make_async_remote_copy(
            src_ref=src, dst_ref=dst, send_sem=send, recv_sem=recv,
            device_id=device, device_id_type=MESH,
        )
        copy.start()
        return copy

    sent = []

    spread = {}
    mine = pl.ds(z * BLOCK + s * 2, 2)
    for q in range(NQ):
        rows = pl.ds(pl.multiple_of(s * SL, SL), SL)
        own = pltpu.make_async_copy(fac.at[:, q, rows, :], gath[q].at[mine], loc_sem.at[q])
        own.start()
        spread[q] = [own]
        for d in range(1, NS):
            to = wrap(s + d, NS)
            rows = pl.ds(pl.multiple_of(to * SL, SL), SL)
            spread[q].append(
                remote(
                    fac.at[:, q, rows, :], gath[q].at[mine],
                    sp_s.at[q, d - 1], sp_r.at[q, d - 1], (z * NS + to, y),
                )
            )
        sent += spread[q][1:]

    first = occ[orb[0, p]]
    second = occ[orb[1, p]]
    row = virt[pl.ds(screen[core * ROWS + y, p], 1), :] - first
    row = jnp.transpose(jnp.broadcast_to(row, (TILE, TILE)))

    def denominator(j, _):
        col = virt[pl.ds(screen[j, p], 1), :] - second
        rec[j] = 1.0 / (row + col)
        return 0

    lax.fori_loop(0, K, denominator, 0)

    ring = {}

    def gather_step(q, t):
        if t == 1:
            spread[q][0].wait()
            for copy in spread[q][1:]:
                copy.wait_recv()
        for way in range(2):
            if t > 1:
                ring[q, t - 1, way].wait_recv()
            if way == 0:
                start, to = wrap(z - (t - 1), NZ) * BLOCK, z_up
            else:
                start, to = wrap(z + (t - 1), NZ) * BLOCK, z_down
            count = BLOCK
            if t == NZ // 2:
                count = BLOCK // 2
                start = start + way * count
            block = gath[q].at[pl.ds(start, count)]
            ring[q, t, way] = remote(
                block, block, ag_s.at[q, t - 1, way], ag_r.at[q, t - 1, way], (to, y)
            )
            sent.append(ring[q, t, way])

    delivered = {}

    def deliver(q):
        for way in range(2):
            ring[q, NZ // 2, way].wait_recv()
        lanes = pl.ds(q * TILE, TILE)
        rows = pl.ds(pl.multiple_of(s * SL, SL), SL)
        for dx in (2, 1, 3, 0):
            to = wrap(x + dx, NX)
            its_pair = z * NX + to

            def pick(k, _):
                value = gath[q][slot_of[screen[k, its_pair]]]
                if dx == 0:
                    tiles[k, rows, lanes] = value
                else:
                    sel[q, dx - 1, k] = value
                return 0

            lax.fori_loop(0, K, pick, 0, unroll=4)
            if dx:
                delivered[q, dx] = remote(
                    sel.at[q, dx - 1], tiles.at[:, rows, lanes],
                    dl_s.at[q, dx - 1], dl_r.at[q, dx - 1], (z * NS + to * NC + core, y),
                )
                sent.append(delivered[q, dx])

    exchanged = {}

    def exchange(q):
        lanes = pl.ds(q * TILE, TILE)
        for dx in (0, 1, 3, 2):
            if dx:
                delivered[q, dx].wait_recv()
            rows = pl.ds(pl.multiple_of((wrap(x - dx, NX) * NC + core) * SL, SL), SL)
            block = tiles.at[:, rows, lanes]
            exchanged[q, dx] = remote(
                block, block, ex_s.at[q, dx], ex_r.at[q, dx], (z * NS + x * NC + 1 - core, y)
            )
            sent.append(exchanged[q, dx])

    def first_product(q):
        for dx in range(NX):
            exchanged[q, dx].wait_recv()
        lanes = pl.ds(q * TILE, TILE)

        def one_row(i, _):
            left = tiles[core * ROWS + i, :, lanes]
            rows = pl.ds(pl.multiple_of(i * TILE, TILE), TILE)
            for c in range(4):
                value = jnp.dot(
                    left, a_buf[rows, c * 512 : (c + 1) * 512], preferred_element_type=F32
                ).astype(BF16)
                for jj in range(4):
                    half[i, c * 4 + jj, :, lanes] = value[:, jj * TILE : (jj + 1) * TILE]
            return 0

        lax.fori_loop(0, ROWS, one_row, 0)

    for q, t in GATHER_ORDER:
        gather_step(q, t)
        if (q, t) == (1, 3):
            deliver(0)
        if (q, t) == (2, 2):
            exchange(0)
        if (q, t) == (2, 3):
            deliver(1)
    load_a.wait()
    first_product(0)
    exchange(1)
    deliver(2)
    first_product(1)
    exchange(2)
    first_product(2)

    def partial(r, slot):
        def one_column(j, _):
            part[slot, j] = lax.dot_general(
                half[r, j], tiles[j], (((1,), (1,)), ((), ())), preferred_element_type=F32
            )
            return 0

        lax.fori_loop(0, K, one_column, 0, unroll=2)

    moved = {}

    def send(way, t, sub, slot, add):
        value = part[slot, sub * SJ : (sub + 1) * SJ]
        if add:
            moved[way, t - 1, sub].wait_recv()
            value = value + rcv[way, t - 2, sub].astype(F32)
        snd[way, t - 1, sub] = value.astype(BF16)
        moved[way, t, sub] = remote(
            snd.at[way, t - 1, sub], rcv.at[way, t - 1, sub],
            rs_s.at[way, t - 1, sub], rs_r.at[way, t - 1, sub],
            (pair, y_up if way == 0 else y_down),
        )
        sent.append(moved[way, t, sub])

    long_subs = ((0, 1), (2, 3))
    short_subs = ((2, 3), (0, 1))
    partial(wrap(y + 4, NY), 0)
    for n in range(2):
        for way in range(2):
            send(way, 1, long_subs[way][n], 0, False)
    for t in range(2, 5):
        partial(wrap(y + 5 - t, NY), 0)
        partial(wrap(y - 5 + t, NY), 1)
        for n in range(2):
            for way in range(2):
                send(way, t, short_subs[way][n], way, t > 2)
        for n in range(2):
            for way in range(2):
                send(way, t, long_subs[way][n], way, True)
    partial(y, 0)
    for n in (2, 0, 3, 1):
        for way in range(2):
            moved[way, 4, n].wait_recv()
        for j in range(n * SJ, (n + 1) * SJ):
            value = part[0, j] + rcv[0, 3, n, j - n * SJ].astype(F32)
            value = value + rcv[1, 3, n, j - n * SJ].astype(F32)
            out[:, j * TILE : (j + 1) * TILE] = value * rec[j]
    for copy in sent:
        copy.wait_send()


def local(
    amplitudes, factors, screening, tile_slot, pair_orbitals, occupied_energy, virtual_energy
):
    anywhere = pl.BlockSpec(memory_space=pl.ANY)
    smem = pl.BlockSpec(memory_space=pltpu.SMEM)
    vmem = pl.BlockSpec(memory_space=pltpu.VMEM)
    dma = pltpu.SemaphoreType.DMA
    return pl.pallas_call(
        ladder_kernel,
        out_shape=jax.ShapeDtypeStruct((TILE, K * TILE), F32),
        in_specs=[anywhere, anywhere, smem, smem, smem, smem, vmem],
        out_specs=vmem,
        scratch_shapes=[
            pltpu.VMEM((ROWS * TILE, K * TILE), BF16),
            pltpu.VMEM((SLOTS, SL, TILE), BF16),
            pltpu.VMEM((SLOTS, SL, TILE), BF16),
            pltpu.VMEM((SLOTS, SL, TILE), BF16),
            pltpu.VMEM((NQ, NX - 1, K, SL, TILE), BF16),
            pltpu.VMEM((K, TILE, NQ * TILE), BF16),
            pltpu.VMEM((ROWS, K, TILE, NQ * TILE), BF16),
            pltpu.VMEM((2, K, TILE, TILE), F32),
            pltpu.VMEM((2, 4, SUBS, SJ, TILE, TILE), BF16),
            pltpu.VMEM((2, 4, SUBS, SJ, TILE, TILE), BF16),
            pltpu.VMEM((K, TILE, TILE), F32),
            dma,
            dma((NQ,)),
            dma((NQ, NS - 1)),
            dma((NQ, NS - 1)),
            dma((NQ, 4, 2)),
            dma((NQ, 4, 2)),
            dma((NQ, NX - 1)),
            dma((NQ, NX - 1)),
            dma((NQ, NX)),
            dma((NQ, NX)),
            dma((2, 4, SUBS)),
            dma((2, 4, SUBS)),
        ],
        compiler_params=pltpu.CompilerParams(
            collective_id=0, has_side_effects=True, vmem_limit_bytes=48 * 1024 * 1024
        ),
    )(
        amplitudes, factors, screening.T, tile_slot, pair_orbitals.T, occupied_energy, virtual_energy
    )


def solution(mesh):
    return jax.shard_map(
        local,
        mesh=mesh,
        in_specs=(P("pair", None), P("pair", "cuts", None, None), P(), P(), P(), P(), P()),
        out_specs=P(("pair", "cuts"), None),
        check_vma=False,
    )
```

```python
import jax
import jax.numpy as jnp
from jax import lax
from jax.experimental import pallas as pl
from jax.experimental.pallas import tpu as pltpu
from jax.sharding import PartitionSpec as P

TILE = 128
K = 16
NQ = 3
NZ, NX, NC, NY = 8, 4, 2, 8
NS = NX * NC
SL = TILE // NS
SLOTS = 128
PAIRS = 32
NOCC = 4000
BLOCK = SLOTS // NZ
ROWS = 8
SUBS = 4
SJ = K // SUBS
BF16 = jnp.bfloat16
F32 = jnp.float32
MESH = pl.DeviceIdType.MESH

GATHER_ORDER = sorted(
    [(q, t) for q in range(NQ) for t in range(1, 5)], key=lambda a: a[1] + 0.1 * a[0]
)


def ladder_kernel(
    amp, fac, screen_in, slot_in, orb_in, occ_in, virt_in, out,
    a_buf, gath0, gath1, gath2, sel, tiles, half, part, snd, rcv, rec,
    screen, slot_of, orb, occ, virt, a_sem, in_sem, loc_sem, sp_s, sp_r, ag_s, ag_r, dl_s, dl_r, ex_s, ex_r, rs_s, rs_r,
):
    gath = (gath0, gath1, gath2)
    pair = lax.axis_index("pair")
    y = lax.axis_index("cuts")
    s = lax.rem(pair, NS)
    z = pair // NS
    x = s // NC
    core = lax.rem(s, NC)
    p = pair // NC

    def wrap(value, n):
        return lax.rem(value + n, n)

    z_up, z_down = wrap(z + 1, NZ) * NS + s, wrap(z - 1, NZ) * NS + s
    y_up, y_down = wrap(y + 1, NY), wrap(y - 1, NY)

    load_a = pltpu.make_async_copy(amp, a_buf, a_sem)
    load_a.start()
    loads = [
        pltpu.make_async_copy(src, dst, in_sem.at[n])
        for n, (src, dst) in enumerate(
            ((screen_in, screen), (slot_in, slot_of), (orb_in, orb), (occ_in, occ), (virt_in, virt))
        )
    ]
    for load in loads:
        load.start()

    barrier = pltpu.get_barrier_semaphore()
    peers = [(z * NS + wrap(s + d, NS), y) for d in range(1, NS)]
    peers += [(z_up, y), (z_down, y), (pair, y_up), (pair, y_down)]
    for peer in peers:
        pl.semaphore_signal(barrier, inc=1, device_id=peer, device_id_type=MESH)
    pl.semaphore_wait(barrier, len(peers))

    def remote(src, dst, send, recv, device):
        copy = pltpu.make_async_remote_copy(
            src_ref=src, dst_ref=dst, send_sem=send, recv_sem=recv,
            device_id=device, device_id_type=MESH,
        )
        copy.start()
        return copy

    sent = []

    spread = {}
    mine = pl.ds(z * BLOCK + s * 2, 2)
    for q in range(NQ):
        rows = pl.ds(pl.multiple_of(s * SL, SL), SL)
        own = pltpu.make_async_copy(fac.at[:, q, rows, :], gath[q].at[mine], loc_sem.at[q])
        own.start()
        spread[q] = [own]
        for d in range(1, NS):
            to = wrap(s + d, NS)
            rows = pl.ds(pl.multiple_of(to * SL, SL), SL)
            spread[q].append(
                remote(
                    fac.at[:, q, rows, :], gath[q].at[mine],
                    sp_s.at[q, d - 1], sp_r.at[q, d - 1], (z * NS + to, y),
                )
            )
        sent += spread[q][1:]

    for load in loads:
        load.wait()
    first = occ[orb[0, p]]
    second = occ[orb[1, p]]
    row = virt[pl.ds(screen[core * ROWS + y, p], 1), :] - first
    row = jnp.transpose(jnp.broadcast_to(row, (TILE, TILE)))

    def denominator(j, _):
        col = virt[pl.ds(screen[j, p], 1), :] - second
        rec[j] = 1.0 / (row + col)
        return 0

    lax.fori_loop(0, K, denominator, 0)

    ring = {}

    def gather_step(q, t):
        if t == 1:
            spread[q][0].wait()
            for copy in spread[q][1:]:
                copy.wait_recv()
        for way in range(2):
            if t > 1:
                ring[q, t - 1, way].wait_recv()
            if way == 0:
                start, to = wrap(z - (t - 1), NZ) * BLOCK, z_up
            else:
                start, to = wrap(z + (t - 1), NZ) * BLOCK, z_down
            count = BLOCK
            if t == NZ // 2:
                count = BLOCK // 2
                start = start + way * count
            block = gath[q].at[pl.ds(start, count)]
            ring[q, t, way] = remote(
                block, block, ag_s.at[q, t - 1, way], ag_r.at[q, t - 1, way], (to, y)
            )
            sent.append(ring[q, t, way])

    delivered = {}

    def deliver(q):
        for way in range(2):
            ring[q, NZ // 2, way].wait_recv()
        lanes = pl.ds(q * TILE, TILE)
        rows = pl.ds(pl.multiple_of(s * SL, SL), SL)
        for dx in (2, 1, 3, 0):
            to = wrap(x + dx, NX)
            its_pair = z * NX + to

            def pick(k, _):
                value = gath[q][slot_of[screen[k, its_pair]]]
                if dx == 0:
                    tiles[k, rows, lanes] = value
                else:
                    sel[q, dx - 1, k] = value
                return 0

            lax.fori_loop(0, K, pick, 0, unroll=4)
            if dx:
                delivered[q, dx] = remote(
                    sel.at[q, dx - 1], tiles.at[:, rows, lanes],
                    dl_s.at[q, dx - 1], dl_r.at[q, dx - 1], (z * NS + to * NC + core, y),
                )
                sent.append(delivered[q, dx])

    exchanged = {}

    def exchange(q):
        lanes = pl.ds(q * TILE, TILE)
        for dx in (0, 1, 3, 2):
            if dx:
                delivered[q, dx].wait_recv()
            rows = pl.ds(pl.multiple_of((wrap(x - dx, NX) * NC + core) * SL, SL), SL)
            block = tiles.at[:, rows, lanes]
            exchanged[q, dx] = remote(
                block, block, ex_s.at[q, dx], ex_r.at[q, dx], (z * NS + x * NC + 1 - core, y)
            )
            sent.append(exchanged[q, dx])

    def first_product(q):
        for dx in range(NX):
            exchanged[q, dx].wait_recv()
        lanes = pl.ds(q * TILE, TILE)

        def one_row(i, _):
            left = tiles[core * ROWS + i, :, lanes]
            rows = pl.ds(pl.multiple_of(i * TILE, TILE), TILE)
            for c in range(4):
                value = jnp.dot(
                    left, a_buf[rows, c * 512 : (c + 1) * 512], preferred_element_type=F32
                ).astype(BF16)
                for jj in range(4):
                    half[i, c * 4 + jj, :, lanes] = value[:, jj * TILE : (jj + 1) * TILE]
            return 0

        lax.fori_loop(0, ROWS, one_row, 0)

    for q, t in GATHER_ORDER:
        gather_step(q, t)
    for q in range(NQ):
        deliver(q)
    load_a.wait()
    for q in range(NQ):
        exchange(q)
        if q:
            first_product(q - 1)
    first_product(NQ - 1)

    def partial(r, slot):
        def one_column(j, _):
            part[slot, j] = lax.dot_general(
                half[r, j], tiles[j], (((1,), (1,)), ((), ())), preferred_element_type=F32
            )
            return 0

        lax.fori_loop(0, K, one_column, 0, unroll=2)

    moved = {}

    def send(way, t, sub, slot, add):
        value = part[slot, sub * SJ : (sub + 1) * SJ]
        if add:
            moved[way, t - 1, sub].wait_recv()
            value = value + rcv[way, t - 2, sub].astype(F32)
        snd[way, t - 1, sub] = value.astype(BF16)
        moved[way, t, sub] = remote(
            snd.at[way, t - 1, sub], rcv.at[way, t - 1, sub],
            rs_s.at[way, t - 1, sub], rs_r.at[way, t - 1, sub],
            (pair, y_up if way == 0 else y_down),
        )
        sent.append(moved[way, t, sub])

    long_subs = ((0, 1), (2, 3))
    short_subs = ((2, 3), (0, 1))
    partial(wrap(y + 4, NY), 0)
    for n in range(2):
        for way in range(2):
            send(way, 1, long_subs[way][n], 0, False)
    for t in range(2, 5):
        partial(wrap(y + 5 - t, NY), 0)
        partial(wrap(y - 5 + t, NY), 1)
        for n in range(2):
            for way in range(2):
                send(way, t, short_subs[way][n], way, t > 2)
        for n in range(2):
            for way in range(2):
                send(way, t, long_subs[way][n], way, True)
    partial(y, 0)
    for n in (2, 0, 3, 1):
        for way in range(2):
            moved[way, 4, n].wait_recv()
        for j in range(n * SJ, (n + 1) * SJ):
            value = part[0, j] + rcv[0, 3, n, j - n * SJ].astype(F32)
            value = value + rcv[1, 3, n, j - n * SJ].astype(F32)
            out[:, j * TILE : (j + 1) * TILE] = value * rec[j]
    for copy in sent:
        copy.wait_send()


def local(
    amplitudes, factors, screening, tile_slot, pair_orbitals, occupied_energy, virtual_energy
):
    hbm = pl.BlockSpec(memory_space=pltpu.HBM)
    vmem = pl.BlockSpec(memory_space=pltpu.VMEM)
    dma = pltpu.SemaphoreType.DMA
    return pl.pallas_call(
        ladder_kernel,
        out_shape=jax.ShapeDtypeStruct((TILE, K * TILE), F32),
        in_specs=[hbm] * 7,
        out_specs=vmem,
        scratch_shapes=[
            pltpu.VMEM((ROWS * TILE, K * TILE), BF16),
            pltpu.VMEM((SLOTS, SL, TILE), BF16),
            pltpu.VMEM((SLOTS, SL, TILE), BF16),
            pltpu.VMEM((SLOTS, SL, TILE), BF16),
            pltpu.VMEM((NQ, NX - 1, K, SL, TILE), BF16),
            pltpu.VMEM((K, TILE, NQ * TILE), BF16),
            pltpu.VMEM((ROWS, K, TILE, NQ * TILE), BF16),
            pltpu.VMEM((2, K, TILE, TILE), F32),
            pltpu.VMEM((2, 4, SUBS, SJ, TILE, TILE), BF16),
            pltpu.VMEM((2, 4, SUBS, SJ, TILE, TILE), BF16),
            pltpu.VMEM((K, TILE, TILE), F32),
            pltpu.SMEM((K, PAIRS), jnp.int32),
            pltpu.SMEM((SLOTS,), jnp.int32),
            pltpu.SMEM((2, PAIRS), jnp.int32),
            pltpu.SMEM((NOCC,), F32),
            pltpu.VMEM((SLOTS, TILE), F32),
            dma,
            dma((5,)),
            dma((NQ,)),
            dma((NQ, NS - 1)),
            dma((NQ, NS - 1)),
            dma((NQ, 4, 2)),
            dma((NQ, 4, 2)),
            dma((NQ, NX - 1)),
            dma((NQ, NX - 1)),
            dma((NQ, NX)),
            dma((NQ, NX)),
            dma((2, 4, SUBS)),
            dma((2, 4, SUBS)),
        ],
        compiler_params=pltpu.CompilerParams(
            collective_id=0, has_side_effects=True, vmem_limit_bytes=60 * 1024 * 1024
        ),
    )(
        amplitudes, factors, screening.T, tile_slot, pair_orbitals.T, occupied_energy, virtual_energy
    )


def solution(mesh):
    return jax.shard_map(
        local,
        mesh=mesh,
        in_specs=(P("pair", None), P("pair", "cuts", None, None), P(), P(), P(), P(), P()),
        out_specs=P(("pair", "cuts"), None),
        check_vma=False,
    )
```

```python
import jax
import jax.numpy as jnp
from jax import lax
from jax.experimental import pallas as pl
from jax.experimental.pallas import tpu as pltpu
from jax.sharding import PartitionSpec as P

TILE = 128
K = 16
NQ = 3
NZ, NX, NC, NY = 8, 4, 2, 8
NS = NX * NC
SL = TILE // NS
SLOTS = 128
PAIRS = 32
NOCC = 4000
BLOCK = SLOTS // NZ
ROWS = 8
SUBS = 4
SJ = K // SUBS
LEAD = NY // 2
BF16 = jnp.bfloat16
F32 = jnp.float32
MESH = pl.DeviceIdType.MESH

SCHEDULE = (
    ("g", 0, 1), ("g", 1, 1), ("g", 2, 1), ("g", 0, 2), ("g", 1, 2), ("g", 0, 3),
    ("g", 2, 2), ("g", 0, 4), ("g", 1, 3), ("g", 2, 3), ("d", 0, 0), ("g", 1, 4),
    ("g", 2, 4), ("d", 1, 0), ("e", 0, 0), ("d", 2, 0),
)


def ladder_kernel(
    amp, fac, screen_in, slot_in, orb_in, occ_in, virt_in, out,
    a_buf, gath0, gath1, gath2, sel, tiles, half, part, snd, rcv, rec,
    screen, slot_of, wanted, orb, occ, virt, a_sem, in_sem, loc_sem, sp_s, sp_r, ag_s, ag_r, dl_s, dl_r, ex_s, ex_r, rs_s, rs_r,
):
    gath = (gath0, gath1, gath2)
    pair = lax.axis_index("pair")
    y = lax.axis_index("cuts")
    s = lax.rem(pair, NS)
    z = pair // NS
    x = s // NC
    core = lax.rem(s, NC)
    p = pair // NC

    def wrap(value, n):
        return lax.rem(value + n, n)

    z_up, z_down = wrap(z + 1, NZ) * NS + s, wrap(z - 1, NZ) * NS + s
    y_up, y_down = wrap(y + 1, NY), wrap(y - 1, NY)

    load_a = pltpu.make_async_copy(amp, a_buf, a_sem)
    load_a.start()
    loads = [
        pltpu.make_async_copy(src, dst, in_sem.at[n])
        for n, (src, dst) in enumerate(
            ((screen_in, screen), (slot_in, slot_of), (orb_in, orb), (occ_in, occ), (virt_in, virt))
        )
    ]
    for load in loads:
        load.start()

    barrier = pltpu.get_barrier_semaphore()
    peers = [(z * NS + wrap(s + d, NS), y) for d in range(1, NS)]
    peers += [(z_up, y), (z_down, y), (pair, y_up), (pair, y_down)]
    for peer in peers:
        pl.semaphore_signal(barrier, inc=1, device_id=peer, device_id_type=MESH)
    pl.semaphore_wait(barrier, len(peers))

    def remote(src, dst, send, recv, device):
        copy = pltpu.make_async_remote_copy(
            src_ref=src, dst_ref=dst, send_sem=send, recv_sem=recv,
            device_id=device, device_id_type=MESH,
        )
        copy.start()
        return copy

    sent = []

    spread = {}
    mine = pl.ds(z * BLOCK + s * 2, 2)
    for q in range(NQ):
        rows = pl.ds(pl.multiple_of(s * SL, SL), SL)
        own = pltpu.make_async_copy(fac.at[:, q, rows, :], gath[q].at[mine], loc_sem.at[q])
        own.start()
        spread[q] = [own]
        for d in range(1, NS):
            to = wrap(s + d, NS)
            rows = pl.ds(pl.multiple_of(to * SL, SL), SL)
            spread[q].append(
                remote(
                    fac.at[:, q, rows, :], gath[q].at[mine],
                    sp_s.at[q, d - 1], sp_r.at[q, d - 1], (z * NS + to, y),
                )
            )
        sent += spread[q][1:]

    for load in loads:
        load.wait()
    for dx in range(NX):

        def want(k, _):
            wanted[dx, k] = slot_of[screen[k, z * NX + wrap(x + dx, NX)]]
            return 0

        lax.fori_loop(0, K, want, 0)
    first = occ[orb[0, p]]
    second = occ[orb[1, p]]
    row = virt[pl.ds(screen[core * ROWS + y, p], 1), :] - first
    row = jnp.transpose(jnp.broadcast_to(row, (TILE, TILE)))

    def denominator(j, _):
        col = virt[pl.ds(screen[j, p], 1), :] - second
        rec[j] = 1.0 / (row + col)
        return 0

    lax.fori_loop(0, K, denominator, 0)

    ring = {}

    def gather_step(q, t):
        if t == 1:
            spread[q][0].wait()
            for copy in spread[q][1:]:
                copy.wait_recv()
        for way in range(2):
            if t > 1:
                ring[q, t - 1, way].wait_recv()
            if way == 0:
                start, to = wrap(z - (t - 1), NZ) * BLOCK, z_up
            else:
                start, to = wrap(z + (t - 1), NZ) * BLOCK, z_down
            count = BLOCK
            if t == NZ // 2:
                count = BLOCK // 2
                start = start + way * count
            block = gath[q].at[pl.ds(start, count)]
            ring[q, t, way] = remote(
                block, block, ag_s.at[q, t - 1, way], ag_r.at[q, t - 1, way], (to, y)
            )
            sent.append(ring[q, t, way])

    delivered = {}

    def deliver(q):
        for way in range(2):
            ring[q, NZ // 2, way].wait_recv()
        lanes = pl.ds(q * TILE, TILE)
        rows = pl.ds(pl.multiple_of(s * SL, SL), SL)
        for dx in (2, 1, 3, 0):
            to = wrap(x + dx, NX)
            for k in range(K):
                value = gath[q][wanted[dx, k]]
                if dx == 0:
                    tiles[k, rows, lanes] = value
                else:
                    sel[q, dx - 1, k] = value
            if dx:
                delivered[q, dx] = remote(
                    sel.at[q, dx - 1], tiles.at[:, rows, lanes],
                    dl_s.at[q, dx - 1], dl_r.at[q, dx - 1], (z * NS + to * NC + core, y),
                )
                sent.append(delivered[q, dx])

    exchanged = {}

    def exchange(q):
        lanes = pl.ds(q * TILE, TILE)
        for dx in (0, 1, 3, 2):
            if dx:
                delivered[q, dx].wait_recv()
            rows = pl.ds(pl.multiple_of((wrap(x - dx, NX) * NC + core) * SL, SL), SL)
            block = tiles.at[:, rows, lanes]
            exchanged[q, dx] = remote(
                block, block, ex_s.at[q, dx], ex_r.at[q, dx], (z * NS + x * NC + 1 - core, y)
            )
            sent.append(exchanged[q, dx])

    def first_product(q, start=0, count=ROWS):
        if start == 0:
            for dx in range(NX):
                exchanged[q, dx].wait_recv()
        lanes = pl.ds(q * TILE, TILE)

        def one_row(n, _):
            i = wrap(y + LEAD + n, ROWS)
            left = tiles[core * ROWS + i, :, lanes]
            rows = pl.ds(pl.multiple_of(i * TILE, TILE), TILE)
            for c in range(4):
                value = jnp.dot(
                    left, a_buf[rows, c * 512 : (c + 1) * 512], preferred_element_type=F32
                ).astype(BF16)
                for jj in range(4):
                    half[i, c * 4 + jj, :, lanes] = value[:, jj * TILE : (jj + 1) * TILE]
            return 0

        lax.fori_loop(start, start + count, one_row, 0)

    for step in SCHEDULE:
        if step[0] == "g":
            gather_step(step[1], step[2])
        elif step[0] == "d":
            deliver(step[1])
        else:
            exchange(step[1])
    load_a.wait()
    first_product(0)
    exchange(1)
    first_product(1)
    exchange(2)
    first_product(2, 0, 1)

    def partial(r, slot, start=0, count=K):
        def one_column(j, _):
            part[slot, j] = lax.dot_general(
                half[r, j], tiles[j], (((1,), (1,)), ((), ())), preferred_element_type=F32
            )
            return 0

        lax.fori_loop(start, start + count, one_column, 0, unroll=2)

    moved = {}

    def send(way, t, sub, slot, add):
        value = part[slot, sub * SJ : (sub + 1) * SJ]
        if add:
            moved[way, t - 1, sub].wait_recv()
            value = value + rcv[way, t - 2, sub].astype(F32)
        snd[way, t - 1, sub] = value.astype(BF16)
        moved[way, t, sub] = remote(
            snd.at[way, t - 1, sub], rcv.at[way, t - 1, sub],
            rs_s.at[way, t - 1, sub], rs_r.at[way, t - 1, sub],
            (pair, y_up if way == 0 else y_down),
        )
        sent.append(moved[way, t, sub])

    long_subs = ((0, 1), (2, 3))
    short_subs = ((2, 3), (0, 1))
    for n in range(2):
        for way in range(2):
            sub = long_subs[way][n]
            partial(wrap(y + LEAD, NY), 0, sub * SJ, SJ)
            send(way, 1, sub, 0, False)
    first_product(2, 1, ROWS - 1)
    for t in range(2, 5):
        partial(wrap(y + 5 - t, NY), 0)
        partial(wrap(y - 5 + t, NY), 1)
        for n in range(2):
            for way in range(2):
                send(way, t, short_subs[way][n], way, t > 2)
        for n in range(2):
            for way in range(2):
                send(way, t, long_subs[way][n], way, True)
    partial(y, 0)
    for n in (2, 0, 3, 1):
        for way in range(2):
            moved[way, 4, n].wait_recv()
        for j in range(n * SJ, (n + 1) * SJ):
            value = part[0, j] + rcv[0, 3, n, j - n * SJ].astype(F32)
            value = value + rcv[1, 3, n, j - n * SJ].astype(F32)
            out[:, j * TILE : (j + 1) * TILE] = value * rec[j]
    for copy in sent:
        copy.wait_send()


def local(
    amplitudes, factors, screening, tile_slot, pair_orbitals, occupied_energy, virtual_energy
):
    hbm = pl.BlockSpec(memory_space=pltpu.HBM)
    vmem = pl.BlockSpec(memory_space=pltpu.VMEM)
    dma = pltpu.SemaphoreType.DMA
    return pl.pallas_call(
        ladder_kernel,
        out_shape=jax.ShapeDtypeStruct((TILE, K * TILE), F32),
        in_specs=[hbm] * 7,
        out_specs=vmem,
        scratch_shapes=[
            pltpu.VMEM((ROWS * TILE, K * TILE), BF16),
            pltpu.VMEM((SLOTS, SL, TILE), BF16),
            pltpu.VMEM((SLOTS, SL, TILE), BF16),
            pltpu.VMEM((SLOTS, SL, TILE), BF16),
            pltpu.VMEM((NQ, NX - 1, K, SL, TILE), BF16),
            pltpu.VMEM((K, TILE, NQ * TILE), BF16),
            pltpu.VMEM((ROWS, K, TILE, NQ * TILE), BF16),
            pltpu.VMEM((2, K, TILE, TILE), F32),
            pltpu.VMEM((2, 4, SUBS, SJ, TILE, TILE), BF16),
            pltpu.VMEM((2, 4, SUBS, SJ, TILE, TILE), BF16),
            pltpu.VMEM((K, TILE, TILE), F32),
            pltpu.SMEM((K, PAIRS), jnp.int32),
            pltpu.SMEM((SLOTS,), jnp.int32),
            pltpu.SMEM((NX, K), jnp.int32),
            pltpu.SMEM((2, PAIRS), jnp.int32),
            pltpu.SMEM((NOCC,), F32),
            pltpu.VMEM((SLOTS, TILE), F32),
            dma,
            dma((5,)),
            dma((NQ,)),
            dma((NQ, NS - 1)),
            dma((NQ, NS - 1)),
            dma((NQ, 4, 2)),
            dma((NQ, 4, 2)),
            dma((NQ, NX - 1)),
            dma((NQ, NX - 1)),
            dma((NQ, NX)),
            dma((NQ, NX)),
            dma((2, 4, SUBS)),
            dma((2, 4, SUBS)),
        ],
        compiler_params=pltpu.CompilerParams(
            collective_id=0, has_side_effects=True, vmem_limit_bytes=60 * 1024 * 1024
        ),
    )(
        amplitudes, factors, screening.T, tile_slot, pair_orbitals.T, occupied_energy, virtual_energy
    )


def solution(mesh):
    return jax.shard_map(
        local,
        mesh=mesh,
        in_specs=(P("pair", None), P("pair", "cuts", None, None), P(), P(), P(), P(), P()),
        out_specs=P(("pair", "cuts"), None),
        check_vma=False,
    )
```

```python
import jax
import jax.numpy as jnp
from jax import lax
from jax.experimental import pallas as pl
from jax.experimental.pallas import tpu as pltpu
from jax.sharding import PartitionSpec as P

TILE = 128
K = 16
NQ = 3
NZ, NX, NC, NY = 8, 4, 2, 8
NS = NX * NC
SL = TILE // NS
SLOTS = 128
PAIRS = 32
NOCC = 4000
BLOCK = SLOTS // NZ
ROWS = 8
SUBS = 4
SJ = K // SUBS
LEAD = NY // 2
BF16 = jnp.bfloat16
F32 = jnp.float32
MESH = pl.DeviceIdType.MESH

SCHEDULE = (
    ("g", 0, 1), ("g", 1, 1), ("g", 2, 1), ("g", 0, 2), ("g", 1, 2), ("g", 0, 3),
    ("g", 2, 2), ("g", 0, 4), ("g", 1, 3), ("g", 2, 3), ("d", 0, 0), ("g", 1, 4),
    ("g", 2, 4), ("d", 1, 0), ("e", 0, 0), ("d", 2, 0),
)


def ladder_kernel(
    amp, fac, screen_in, slot_in, orb_in, occ_in, virt_in, out,
    a_buf, gath0, gath1, gath2, sel, tiles, half, part, snd, rcv, rec,
    screen, slot_of, wanted, orb, occ, virt, a_sem, in_sem, loc_sem, sp_s, sp_r, ag_s, ag_r, dl_s, dl_r, ex_s, ex_r, rs_s, rs_r,
):
    gath = (gath0, gath1, gath2)
    pair = lax.axis_index("pair")
    y = lax.axis_index("cuts")
    s = lax.rem(pair, NS)
    z = pair // NS
    x = s // NC
    core = lax.rem(s, NC)
    p = pair // NC

    def wrap(value, n):
        return lax.rem(value + n, n)

    z_up, z_down = wrap(z + 1, NZ) * NS + s, wrap(z - 1, NZ) * NS + s
    y_up, y_down = wrap(y + 1, NY), wrap(y - 1, NY)

    load_a = pltpu.make_async_copy(amp, a_buf, a_sem)
    load_a.start()
    loads = [
        pltpu.make_async_copy(src, dst, in_sem.at[n])
        for n, (src, dst) in enumerate(
            ((screen_in, screen), (slot_in, slot_of), (orb_in, orb), (occ_in, occ), (virt_in, virt))
        )
    ]
    for load in loads:
        load.start()

    barrier = pltpu.get_barrier_semaphore()
    peers = [(z * NS + wrap(s + d, NS), y) for d in range(1, NS)]
    peers += [(z_up, y), (z_down, y), (pair, y_up), (pair, y_down)]
    for peer in peers:
        pl.semaphore_signal(barrier, inc=1, device_id=peer, device_id_type=MESH)
    pl.semaphore_wait(barrier, len(peers))

    def remote(src, dst, send, recv, device):
        copy = pltpu.make_async_remote_copy(
            src_ref=src, dst_ref=dst, send_sem=send, recv_sem=recv,
            device_id=device, device_id_type=MESH,
        )
        copy.start()
        return copy

    sent = []

    spread = {}
    mine = pl.ds(z * BLOCK + s * 2, 2)
    for q in range(NQ):
        rows = pl.ds(pl.multiple_of(s * SL, SL), SL)
        own = pltpu.make_async_copy(fac.at[:, q, rows, :], gath[q].at[mine], loc_sem.at[q])
        own.start()
        spread[q] = [own]
        for d in range(1, NS):
            to = wrap(s + d, NS)
            rows = pl.ds(pl.multiple_of(to * SL, SL), SL)
            spread[q].append(
                remote(
                    fac.at[:, q, rows, :], gath[q].at[mine],
                    sp_s.at[q, d - 1], sp_r.at[q, d - 1], (z * NS + to, y),
                )
            )
        sent += spread[q][1:]

    for load in loads:
        load.wait()
    for dx in range(NX):

        def want(k, _):
            wanted[dx, k] = slot_of[screen[k, z * NX + wrap(x + dx, NX)]]
            return 0

        lax.fori_loop(0, K, want, 0)
    first = occ[orb[0, p]]
    second = occ[orb[1, p]]
    row = virt[pl.ds(screen[core * ROWS + y, p], 1), :] - first
    row = jnp.transpose(jnp.broadcast_to(row, (TILE, TILE)))

    def denominator(j, _):
        col = virt[pl.ds(screen[j, p], 1), :] - second
        rec[j] = 1.0 / (row + col)
        return 0

    lax.fori_loop(0, K, denominator, 0)

    ring = {}

    def gather_step(q, t):
        if t == 1:
            spread[q][0].wait()
            for copy in spread[q][1:]:
                copy.wait_recv()
        for way in range(2):
            if t > 1:
                ring[q, t - 1, way].wait_recv()
            if way == 0:
                start, to = wrap(z - (t - 1), NZ) * BLOCK, z_up
            else:
                start, to = wrap(z + (t - 1), NZ) * BLOCK, z_down
            count = BLOCK
            if t == NZ // 2:
                count = BLOCK // 2
                start = start + way * count
            block = gath[q].at[pl.ds(start, count)]
            ring[q, t, way] = remote(
                block, block, ag_s.at[q, t - 1, way], ag_r.at[q, t - 1, way], (to, y)
            )
            sent.append(ring[q, t, way])

    delivered = {}

    def deliver(q):
        for way in range(2):
            ring[q, NZ // 2, way].wait_recv()
        lanes = pl.ds(q * TILE, TILE)
        rows = pl.ds(pl.multiple_of(s * SL, SL), SL)
        for dx in (2, 1, 3, 0):
            to = wrap(x + dx, NX)
            for k in range(K):
                value = gath[q][wanted[dx, k]]
                if dx == 0:
                    tiles[k, rows, lanes] = value
                else:
                    sel[q, dx - 1, k] = value
            if dx:
                delivered[q, dx] = remote(
                    sel.at[q, dx - 1], tiles.at[:, rows, lanes],
                    dl_s.at[q, dx - 1], dl_r.at[q, dx - 1], (z * NS + to * NC + core, y),
                )
                sent.append(delivered[q, dx])

    exchanged = {}

    def exchange(q):
        lanes = pl.ds(q * TILE, TILE)
        for dx in (0, 1, 3, 2):
            if dx:
                delivered[q, dx].wait_recv()
            rows = pl.ds(pl.multiple_of((wrap(x - dx, NX) * NC + core) * SL, SL), SL)
            block = tiles.at[:, rows, lanes]
            exchanged[q, dx] = remote(
                block, block, ex_s.at[q, dx], ex_r.at[q, dx], (z * NS + x * NC + 1 - core, y)
            )
            sent.append(exchanged[q, dx])

    def first_product(q, start=0, count=ROWS):
        if start == 0:
            for dx in range(NX):
                exchanged[q, dx].wait_recv()
        lanes = pl.ds(q * TILE, TILE)

        def one_row(n, _):
            i = wrap(y + LEAD + n, ROWS)
            left = tiles[core * ROWS + i, :, lanes]
            rows = pl.ds(pl.multiple_of(i * TILE, TILE), TILE)
            for c in range(4):
                value = jnp.dot(
                    left, a_buf[rows, c * 512 : (c + 1) * 512], preferred_element_type=F32
                ).astype(BF16)
                for jj in range(4):
                    half[i, c * 4 + jj, :, lanes] = value[:, jj * TILE : (jj + 1) * TILE]
            return 0

        lax.fori_loop(start, start + count, one_row, 0)

    for step in SCHEDULE:
        if step[0] == "g":
            gather_step(step[1], step[2])
        elif step[0] == "d":
            deliver(step[1])
        else:
            exchange(step[1])
    load_a.wait()
    first_product(0)
    exchange(1)
    first_product(1)
    exchange(2)
    first_product(2, 0, 1)

    def partial(r, slot, start=0, count=K):
        def one_column(j, _):
            part[slot, j] = lax.dot_general(
                half[r, j], tiles[j], (((1,), (1,)), ((), ())), preferred_element_type=F32
            )
            return 0

        lax.fori_loop(start, start + count, one_column, 0, unroll=2)

    moved = {}

    def send(way, t, sub, slot, add):
        value = part[slot, sub * SJ : (sub + 1) * SJ]
        if add:
            moved[way, t - 1, sub].wait_recv()
            value = value + rcv[way, t - 2, sub].astype(F32)
        snd[way, t - 1, sub] = value.astype(BF16)
        moved[way, t, sub] = remote(
            snd.at[way, t - 1, sub], rcv.at[way, t - 1, sub],
            rs_s.at[way, t - 1, sub], rs_r.at[way, t - 1, sub],
            (pair, y_up if way == 0 else y_down),
        )
        sent.append(moved[way, t, sub])

    long_subs = ((0, 1), (2, 3))
    short_subs = ((2, 3), (0, 1))
    for n in range(2):
        for way in range(2):
            sub = long_subs[way][n]
            partial(wrap(y + LEAD, NY), 0, sub * SJ, SJ)
            send(way, 1, sub, 0, False)
    first_product(2, 1, ROWS - 1)
    for t in range(2, 5):
        partial(wrap(y + 5 - t, NY), 0)
        partial(wrap(y - 5 + t, NY), 1)
        for n in range(2):
            for way in range(2):
                send(way, t, short_subs[way][n], way, t > 2)
        for n in range(2):
            for way in range(2):
                send(way, t, long_subs[way][n], way, True)
    partial(y, 0)
    for n in (2, 0, 3, 1):
        for way in range(2):
            moved[way, 4, n].wait_recv()
        for j in range(n * SJ, (n + 1) * SJ):
            value = part[0, j] + rcv[0, 3, n, j - n * SJ].astype(F32)
            value = value + rcv[1, 3, n, j - n * SJ].astype(F32)
            out[:, j * TILE : (j + 1) * TILE] = value * rec[j]
    for copy in sent:
        copy.wait_send()


def local(
    amplitudes, factors, screening, tile_slot, pair_orbitals, occupied_energy, virtual_energy
):
    arrays = (
        amplitudes, factors, screening.T, tile_slot, pair_orbitals.T, occupied_energy, virtual_energy
    )
    hbm = pl.BlockSpec(memory_space=pltpu.HBM)
    dma = pltpu.SemaphoreType.DMA
    return pl.pallas_call(
        ladder_kernel,
        out_shape=jax.ShapeDtypeStruct((TILE, K * TILE), F32),
        in_specs=[hbm] * 7,
        out_specs=pl.BlockSpec(memory_space=pltpu.VMEM),
        scratch_shapes=[
            pltpu.VMEM((ROWS * TILE, K * TILE), BF16),
            pltpu.VMEM((SLOTS, SL, TILE), BF16),
            pltpu.VMEM((SLOTS, SL, TILE), BF16),
            pltpu.VMEM((SLOTS, SL, TILE), BF16),
            pltpu.VMEM((NQ, NX - 1, K, SL, TILE), BF16),
            pltpu.VMEM((K, TILE, NQ * TILE), BF16),
            pltpu.VMEM((ROWS, K, TILE, NQ * TILE), BF16),
            pltpu.VMEM((2, K, TILE, TILE), F32),
            pltpu.VMEM((2, 4, SUBS, SJ, TILE, TILE), BF16),
            pltpu.VMEM((2, 4, SUBS, SJ, TILE, TILE), BF16),
            pltpu.VMEM((K, TILE, TILE), F32),
            pltpu.SMEM((K, PAIRS), jnp.int32),
            pltpu.SMEM((SLOTS,), jnp.int32),
            pltpu.SMEM((NX, K), jnp.int32),
            pltpu.SMEM((2, PAIRS), jnp.int32),
            pltpu.SMEM((NOCC,), F32),
            pltpu.VMEM((SLOTS, TILE), F32),
            dma,
            dma((5,)),
            dma((NQ,)),
            dma((NQ, NS - 1)),
            dma((NQ, NS - 1)),
            dma((NQ, 4, 2)),
            dma((NQ, 4, 2)),
            dma((NQ, NX - 1)),
            dma((NQ, NX - 1)),
            dma((NQ, NX)),
            dma((NQ, NX)),
            dma((2, 4, SUBS)),
            dma((2, 4, SUBS)),
        ],
        compiler_params=pltpu.CompilerParams(
            collective_id=0, has_side_effects=True, vmem_limit_bytes=48 * 1024 * 1024
        ),
    )(*(pltpu.with_memory_space_constraint(array, pltpu.HBM) for array in arrays))


def solution(mesh):
    return jax.shard_map(
        local,
        mesh=mesh,
        in_specs=(P("pair", None), P("pair", "cuts", None, None), P(), P(), P(), P(), P()),
        out_specs=P(("pair", "cuts"), None),
        check_vma=False,
    )
```

```python
import jax
import jax.numpy as jnp
from jax import lax
from jax.experimental import pallas as pl
from jax.experimental.pallas import tpu as pltpu
from jax.sharding import PartitionSpec as P

TILE = 128
K = 16
NQ = 3
NZ, NX, NC, NY = 8, 4, 2, 8
NS = NX * NC
SL = TILE // NS
SLOTS = 128
PAIRS = 32
NOCC = 4000
BLOCK = SLOTS // NZ
ROWS = 8
SUBS = 4
SJ = K // SUBS
LEAD = NY // 2
BF16 = jnp.bfloat16
F32 = jnp.float32
MESH = pl.DeviceIdType.MESH

SCHEDULE = (
    ("g", 0, 1), ("g", 1, 1), ("g", 2, 1), ("g", 0, 2), ("g", 1, 2), ("g", 0, 3),
    ("g", 2, 2), ("g", 0, 4), ("g", 1, 3), ("g", 2, 3), ("d", 0, 0), ("g", 1, 4),
    ("g", 2, 4), ("d", 1, 0), ("e", 0, 0), ("d", 2, 0),
)


def ladder_kernel(
    amp, fac, screen_in, slot_in, orb_in, occ_in, virt_in, out,
    a_buf, gath0, gath1, gath2, sel, tiles, half, part, snd, rcv, rec,
    screen, slot_of, wanted, orb, occ, virt, a_sem, in_sem, loc_sem, sp_s, sp_r, ag_s, ag_r, dl_s, dl_r, ex_s, ex_r, rs_s, rs_r,
):
    gath = (gath0, gath1, gath2)
    pair = lax.axis_index("pair")
    y = lax.axis_index("cuts")
    s = lax.rem(pair, NS)
    z = pair // NS
    x = s // NC
    core = lax.rem(s, NC)
    p = pair // NC

    def wrap(value, n):
        return lax.rem(value + n, n)

    z_up, z_down = wrap(z + 1, NZ) * NS + s, wrap(z - 1, NZ) * NS + s
    y_up, y_down = wrap(y + 1, NY), wrap(y - 1, NY)

    load_a = pltpu.make_async_copy(amp, a_buf, a_sem)
    load_a.start()
    loads = [
        pltpu.make_async_copy(src, dst, in_sem.at[n])
        for n, (src, dst) in enumerate(
            ((screen_in, screen), (slot_in, slot_of), (orb_in, orb), (occ_in, occ), (virt_in, virt))
        )
    ]
    for load in loads:
        load.start()

    barrier = pltpu.get_barrier_semaphore()
    peers = [(z * NS + wrap(s + d, NS), y) for d in range(1, NS)]
    peers += [(z_up, y), (z_down, y), (pair, y_up), (pair, y_down)]
    for peer in peers:
        pl.semaphore_signal(barrier, inc=1, device_id=peer, device_id_type=MESH)
    pl.semaphore_wait(barrier, len(peers))

    def remote(src, dst, send, recv, device):
        copy = pltpu.make_async_remote_copy(
            src_ref=src, dst_ref=dst, send_sem=send, recv_sem=recv,
            device_id=device, device_id_type=MESH,
        )
        copy.start()
        return copy

    sent = []

    spread = {}
    mine = pl.ds(z * BLOCK + s * 2, 2)
    for q in range(NQ):
        rows = pl.ds(pl.multiple_of(s * SL, SL), SL)
        own = pltpu.make_async_copy(fac.at[:, q, rows, :], gath[q].at[mine], loc_sem.at[q])
        own.start()
        spread[q] = [own]
        for d in (4, 3, 5, 2, 6, 1, 7):
            to = wrap(s + d, NS)
            rows = pl.ds(pl.multiple_of(to * SL, SL), SL)
            spread[q].append(
                remote(
                    fac.at[:, q, rows, :], gath[q].at[mine],
                    sp_s.at[q, d - 1], sp_r.at[q, d - 1], (z * NS + to, y),
                )
            )
        sent += spread[q][1:]

    def look_up():
        for load in loads:
            load.wait()
        for dx in range(NX):
            its_pair = z * NX + wrap(x + dx, NX)

            def want(k, _):
                wanted[dx, k] = slot_of[screen[k, its_pair]]
                return 0

            lax.fori_loop(0, K, want, 0, unroll=4)

    def denominators():
        first = occ[orb[0, p]]
        second = occ[orb[1, p]]
        row = virt[pl.ds(screen[core * ROWS + y, p], 1), :] - first
        row = jnp.transpose(jnp.broadcast_to(row, (TILE, TILE)))

        def denominator(j, _):
            col = virt[pl.ds(screen[j, p], 1), :] - second
            rec[j] = 1.0 / (row + col)
            return 0

        lax.fori_loop(0, K, denominator, 0)

    ring = {}

    def gather_step(q, t):
        if t == 1:
            spread[q][0].wait()
            for copy in spread[q][1:]:
                copy.wait_recv()
        for way in range(2):
            if t > 1:
                ring[q, t - 1, way].wait_recv()
            if way == 0:
                start, to = wrap(z - (t - 1), NZ) * BLOCK, z_up
            else:
                start, to = wrap(z + (t - 1), NZ) * BLOCK, z_down
            count = BLOCK
            if t == NZ // 2:
                count = BLOCK // 2
                start = start + way * count
            block = gath[q].at[pl.ds(start, count)]
            ring[q, t, way] = remote(
                block, block, ag_s.at[q, t - 1, way], ag_r.at[q, t - 1, way], (to, y)
            )
            sent.append(ring[q, t, way])

    delivered = {}

    def deliver(q):
        for way in range(2):
            ring[q, NZ // 2, way].wait_recv()
        lanes = pl.ds(q * TILE, TILE)
        rows = pl.ds(pl.multiple_of(s * SL, SL), SL)
        for dx in (2, 1, 3, 0):
            to = wrap(x + dx, NX)
            for k in range(K):
                value = gath[q][wanted[dx, k]]
                if dx == 0:
                    tiles[k, rows, lanes] = value
                else:
                    sel[q, dx - 1, k] = value
            if dx:
                delivered[q, dx] = remote(
                    sel.at[q, dx - 1], tiles.at[:, rows, lanes],
                    dl_s.at[q, dx - 1], dl_r.at[q, dx - 1], (z * NS + to * NC + core, y),
                )
                sent.append(delivered[q, dx])

    exchanged = {}

    def exchange(q):
        lanes = pl.ds(q * TILE, TILE)
        for dx in (0, 1, 3, 2):
            if dx:
                delivered[q, dx].wait_recv()
            rows = pl.ds(pl.multiple_of((wrap(x - dx, NX) * NC + core) * SL, SL), SL)
            block = tiles.at[:, rows, lanes]
            exchanged[q, dx] = remote(
                block, block, ex_s.at[q, dx], ex_r.at[q, dx], (z * NS + x * NC + 1 - core, y)
            )
            sent.append(exchanged[q, dx])

    def first_product(q, start=0, count=ROWS):
        if start == 0:
            for dx in range(NX):
                exchanged[q, dx].wait_recv()
        lanes = pl.ds(q * TILE, TILE)

        def one_row(n, _):
            i = wrap(y + LEAD + n, ROWS)
            left = tiles[core * ROWS + i, :, lanes]
            rows = pl.ds(pl.multiple_of(i * TILE, TILE), TILE)
            for c in range(4):
                value = jnp.dot(
                    left, a_buf[rows, c * 512 : (c + 1) * 512], preferred_element_type=F32
                ).astype(BF16)
                for jj in range(4):
                    half[i, c * 4 + jj, :, lanes] = value[:, jj * TILE : (jj + 1) * TILE]
            return 0

        lax.fori_loop(start, start + count, one_row, 0)

    for step in SCHEDULE:
        if step[0] == "g":
            gather_step(step[1], step[2])
        elif step[0] == "d":
            deliver(step[1])
        else:
            exchange(step[1])
        if step == ("g", 2, 1):
            look_up()
    load_a.wait()
    exchange(1)
    first_product(0)
    exchange(2)
    first_product(1)
    first_product(2, 0, 1)

    def partial(r, slot, start=0, count=K):
        def one_column(j, _):
            part[slot, j] = lax.dot_general(
                half[r, j], tiles[j], (((1,), (1,)), ((), ())), preferred_element_type=F32
            )
            return 0

        lax.fori_loop(start, start + count, one_column, 0, unroll=2)

    moved = {}

    def send(way, t, sub, slot, add):
        value = part[slot, sub * SJ : (sub + 1) * SJ]
        if add:
            moved[way, t - 1, sub].wait_recv()
            value = value + rcv[way, t - 2, sub].astype(F32)
        snd[way, t - 1, sub] = value.astype(BF16)
        moved[way, t, sub] = remote(
            snd.at[way, t - 1, sub], rcv.at[way, t - 1, sub],
            rs_s.at[way, t - 1, sub], rs_r.at[way, t - 1, sub],
            (pair, y_up if way == 0 else y_down),
        )
        sent.append(moved[way, t, sub])

    long_subs = ((0, 1), (2, 3))
    short_subs = ((2, 3), (0, 1))
    for n in range(2):
        for way in range(2):
            sub = long_subs[way][n]
            partial(wrap(y + LEAD, NY), 0, sub * SJ, SJ)
            send(way, 1, sub, 0, False)
    first_product(2, 1, ROWS - 1)
    denominators()
    for t in range(2, 5):
        partial(wrap(y + 5 - t, NY), 0)
        partial(wrap(y - 5 + t, NY), 1)
        for n in range(2):
            for way in range(2):
                send(way, t, short_subs[way][n], way, t > 2)
        for n in range(2):
            for way in range(2):
                send(way, t, long_subs[way][n], way, True)
    partial(y, 0)
    for n in (2, 0, 3, 1):
        for way in range(2):
            moved[way, 4, n].wait_recv()
        for j in range(n * SJ, (n + 1) * SJ):
            value = part[0, j] + rcv[0, 3, n, j - n * SJ].astype(F32)
            value = value + rcv[1, 3, n, j - n * SJ].astype(F32)
            out[:, j * TILE : (j + 1) * TILE] = value * rec[j]
    for copy in sent:
        copy.wait_send()


def local(
    amplitudes, factors, screening, tile_slot, pair_orbitals, occupied_energy, virtual_energy
):
    arrays = (
        amplitudes, factors, screening.T, tile_slot, pair_orbitals.T, occupied_energy, virtual_energy
    )
    hbm = pl.BlockSpec(memory_space=pltpu.HBM)
    dma = pltpu.SemaphoreType.DMA
    return pl.pallas_call(
        ladder_kernel,
        out_shape=jax.ShapeDtypeStruct((TILE, K * TILE), F32),
        in_specs=[hbm] * 7,
        out_specs=pl.BlockSpec(memory_space=pltpu.VMEM),
        scratch_shapes=[
            pltpu.VMEM((ROWS * TILE, K * TILE), BF16),
            pltpu.VMEM((SLOTS, SL, TILE), BF16),
            pltpu.VMEM((SLOTS, SL, TILE), BF16),
            pltpu.VMEM((SLOTS, SL, TILE), BF16),
            pltpu.VMEM((NQ, NX - 1, K, SL, TILE), BF16),
            pltpu.VMEM((K, TILE, NQ * TILE), BF16),
            pltpu.VMEM((ROWS, K, TILE, NQ * TILE), BF16),
            pltpu.VMEM((2, K, TILE, TILE), F32),
            pltpu.VMEM((2, 4, SUBS, SJ, TILE, TILE), BF16),
            pltpu.VMEM((2, 4, SUBS, SJ, TILE, TILE), BF16),
            pltpu.VMEM((K, TILE, TILE), F32),
            pltpu.SMEM((K, PAIRS), jnp.int32),
            pltpu.SMEM((SLOTS,), jnp.int32),
            pltpu.SMEM((NX, K), jnp.int32),
            pltpu.SMEM((2, PAIRS), jnp.int32),
            pltpu.SMEM((NOCC,), F32),
            pltpu.VMEM((SLOTS, TILE), F32),
            dma,
            dma((5,)),
            dma((NQ,)),
            dma((NQ, NS - 1)),
            dma((NQ, NS - 1)),
            dma((NQ, 4, 2)),
            dma((NQ, 4, 2)),
            dma((NQ, NX - 1)),
            dma((NQ, NX - 1)),
            dma((NQ, NX)),
            dma((NQ, NX)),
            dma((2, 4, SUBS)),
            dma((2, 4, SUBS)),
        ],
        compiler_params=pltpu.CompilerParams(
            collective_id=0, has_side_effects=True, vmem_limit_bytes=48 * 1024 * 1024
        ),
    )(*(pltpu.with_memory_space_constraint(array, pltpu.HBM) for array in arrays))


def solution(mesh):
    return jax.shard_map(
        local,
        mesh=mesh,
        in_specs=(P("pair", None), P("pair", "cuts", None, None), P(), P(), P(), P(), P()),
        out_specs=P(("pair", "cuts"), None),
        check_vma=False,
    )
```

```python
import jax
import jax.numpy as jnp
from jax import lax
from jax.experimental import pallas as pl
from jax.experimental.pallas import tpu as pltpu
from jax.sharding import PartitionSpec as P

TILE = 128
K = 16
NQ = 3
NZ, NX, NC, NY = 8, 4, 2, 8
NS = NX * NC
SL = TILE // NS
SLOTS = 128
PAIRS = 32
NOCC = 4000
BLOCK = SLOTS // NZ
ROWS = 8
SUBS = 4
SJ = K // SUBS
LEAD = NY // 2
BF16 = jnp.bfloat16
F32 = jnp.float32
MESH = pl.DeviceIdType.MESH

SCHEDULE = (
    ("g", 0, 1), ("g", 1, 1), ("g", 2, 1), ("g", 0, 2), ("g", 1, 2), ("g", 0, 3),
    ("g", 2, 2), ("g", 0, 4), ("g", 1, 3), ("g", 2, 3), ("d", 0, 0), ("g", 1, 4),
    ("g", 2, 4), ("d", 1, 0), ("e", 0, 0), ("d", 2, 0),
)


def ladder_kernel(
    amp, fac, screen_in, slot_in, orb_in, occ_in, virt_in, out,
    a_buf, gath0, gath1, gath2, sel, tiles, half, part, snd, rcv, rec,
    screen, slot_of, wanted, orb, occ, virt, a_sem, in_sem, loc_sem, sp_s, sp_r, ag_s, ag_r, dl_s, dl_r, ex_s, ex_r, rs_s, rs_r,
):
    gath = (gath0, gath1, gath2)
    pair = lax.axis_index("pair")
    y = lax.axis_index("cuts")
    s = lax.rem(pair, NS)
    z = pair // NS
    x = s // NC
    core = lax.rem(s, NC)
    p = pair // NC

    def wrap(value, n):
        return lax.rem(value + n, n)

    z_up, z_down = wrap(z + 1, NZ) * NS + s, wrap(z - 1, NZ) * NS + s
    y_up, y_down = wrap(y + 1, NY), wrap(y - 1, NY)

    load_a = pltpu.make_async_copy(amp, a_buf, a_sem)
    load_a.start()
    loads = [
        pltpu.make_async_copy(src, dst, in_sem.at[n])
        for n, (src, dst) in enumerate(
            ((screen_in, screen), (slot_in, slot_of), (orb_in, orb), (occ_in, occ), (virt_in, virt))
        )
    ]
    for load in loads:
        load.start()

    barrier = pltpu.get_barrier_semaphore()
    peers = [(z * NS + wrap(s + d, NS), y) for d in range(1, NS)]
    peers += [(z_up, y), (z_down, y), (pair, y_up), (pair, y_down)]
    for peer in peers:
        pl.semaphore_signal(barrier, inc=1, device_id=peer, device_id_type=MESH)
    pl.semaphore_wait(barrier, len(peers))

    def remote(src, dst, send, recv, device):
        copy = pltpu.make_async_remote_copy(
            src_ref=src, dst_ref=dst, send_sem=send, recv_sem=recv,
            device_id=device, device_id_type=MESH,
        )
        copy.start()
        return copy

    sent = []

    spread = {}
    mine = pl.ds(z * BLOCK + s * 2, 2)
    for q in range(NQ):
        rows = pl.ds(pl.multiple_of(s * SL, SL), SL)
        own = pltpu.make_async_copy(fac.at[:, q, rows, :], gath[q].at[mine], loc_sem.at[q])
        own.start()
        spread[q] = [own]
        for d in (4, 3, 5, 2, 6, 1, 7):
            to = wrap(s + d, NS)
            rows = pl.ds(pl.multiple_of(to * SL, SL), SL)
            spread[q].append(
                remote(
                    fac.at[:, q, rows, :], gath[q].at[mine],
                    sp_s.at[q, d - 1], sp_r.at[q, d - 1], (z * NS + to, y),
                )
            )
        sent += spread[q][1:]

    def look_up():
        for load in loads:
            load.wait()
        for dx in range(NX):
            its_pair = z * NX + wrap(x + dx, NX)

            def want(k, _):
                wanted[dx, k] = slot_of[screen[k, its_pair]]
                return 0

            lax.fori_loop(0, K, want, 0, unroll=4)

    def denominators():
        first = occ[orb[0, p]]
        second = occ[orb[1, p]]
        row = virt[pl.ds(screen[core * ROWS + y, p], 1), :] - first
        row = jnp.transpose(jnp.broadcast_to(row, (TILE, TILE)))

        def denominator(j, _):
            col = virt[pl.ds(screen[j, p], 1), :] - second
            rec[j] = 1.0 / (row + col)
            return 0

        lax.fori_loop(0, K, denominator, 0)

    ring = {}

    def gather_step(q, t):
        if t == 1:
            spread[q][0].wait()
            for copy in spread[q][1:]:
                copy.wait_recv()
        for way in range(2):
            if t > 1:
                ring[q, t - 1, way].wait_recv()
            if way == 0:
                start, to = wrap(z - (t - 1), NZ) * BLOCK, z_up
            else:
                start, to = wrap(z + (t - 1), NZ) * BLOCK, z_down
            count = BLOCK
            if t == NZ // 2:
                count = BLOCK // 2
                start = start + way * count
            block = gath[q].at[pl.ds(start, count)]
            ring[q, t, way] = remote(
                block, block, ag_s.at[q, t - 1, way], ag_r.at[q, t - 1, way], (to, y)
            )
            sent.append(ring[q, t, way])

    delivered = {}

    def deliver(q):
        for way in range(2):
            ring[q, NZ // 2, way].wait_recv()
        lanes = pl.ds(q * TILE, TILE)
        rows = pl.ds(pl.multiple_of(s * SL, SL), SL)
        for dx in (2, 1, 3, 0):
            to = wrap(x + dx, NX)
            for k in range(K):
                value = gath[q][wanted[dx, k]]
                if dx == 0:
                    tiles[k, rows, lanes] = value
                else:
                    sel[q, dx - 1, k] = value
            if dx:
                delivered[q, dx] = remote(
                    sel.at[q, dx - 1], tiles.at[:, rows, lanes],
                    dl_s.at[q, dx - 1], dl_r.at[q, dx - 1], (z * NS + to * NC + core, y),
                )
                sent.append(delivered[q, dx])

    exchanged = {}

    def exchange(q):
        lanes = pl.ds(q * TILE, TILE)
        for dx in (0, 1, 3, 2):
            if dx:
                delivered[q, dx].wait_recv()
            rows = pl.ds(pl.multiple_of((wrap(x - dx, NX) * NC + core) * SL, SL), SL)
            block = tiles.at[:, rows, lanes]
            exchanged[q, dx] = remote(
                block, block, ex_s.at[q, dx], ex_r.at[q, dx], (z * NS + x * NC + 1 - core, y)
            )
            sent.append(exchanged[q, dx])

    def first_product(q, start=0, count=ROWS):
        if start == 0:
            for dx in range(NX):
                exchanged[q, dx].wait_recv()
        lanes = pl.ds(q * TILE, TILE)

        def one_row(n, _):
            i = wrap(y + LEAD + n, ROWS)
            left = tiles[core * ROWS + i, :, lanes]
            rows = pl.ds(pl.multiple_of(i * TILE, TILE), TILE)
            for c in range(4):
                value = jnp.dot(
                    left, a_buf[rows, c * 512 : (c + 1) * 512], preferred_element_type=F32
                ).astype(BF16)
                for jj in range(4):
                    half[i, c * 4 + jj, :, lanes] = value[:, jj * TILE : (jj + 1) * TILE]
            return 0

        lax.fori_loop(start, start + count, one_row, 0)

    for step in SCHEDULE:
        if step[0] == "g":
            gather_step(step[1], step[2])
        elif step[0] == "d":
            deliver(step[1])
        else:
            exchange(step[1])
        if step == ("g", 2, 1):
            look_up()
    load_a.wait()
    exchange(1)
    first_product(0)
    exchange(2)
    first_product(1)
    first_product(2, 0, 1)

    def partial(r, slot, start=0, count=K):
        def one_column(j, _):
            part[slot, j] = lax.dot_general(
                half[r, j], tiles[j], (((1,), (1,)), ((), ())), preferred_element_type=F32
            )
            return 0

        lax.fori_loop(start, start + count, one_column, 0, unroll=4)

    moved = {}

    def send(way, t, sub, slot, add):
        value = part[slot, sub * SJ : (sub + 1) * SJ]
        if add:
            moved[way, t - 1, sub].wait_recv()
            value = value + rcv[way, t - 2, sub].astype(F32)
        snd[way, t - 1, sub] = value.astype(BF16)
        moved[way, t, sub] = remote(
            snd.at[way, t - 1, sub], rcv.at[way, t - 1, sub],
            rs_s.at[way, t - 1, sub], rs_r.at[way, t - 1, sub],
            (pair, y_up if way == 0 else y_down),
        )
        sent.append(moved[way, t, sub])

    long_subs = ((0, 1), (2, 3))
    short_subs = ((2, 3), (0, 1))
    for n in range(2):
        for way in range(2):
            sub = long_subs[way][n]
            partial(wrap(y + LEAD, NY), 0, sub * SJ, SJ)
            send(way, 1, sub, 0, False)
    first_product(2, 1, ROWS - 1)
    denominators()
    for t in range(2, 5):
        partial(wrap(y + 5 - t, NY), 0)
        partial(wrap(y - 5 + t, NY), 1)
        for n in range(2):
            for way in range(2):
                send(way, t, short_subs[way][n], way, t > 2)
        for n in range(2):
            for way in range(2):
                send(way, t, long_subs[way][n], way, True)
    partial(y, 0)
    for n in (2, 0, 3, 1):
        for way in range(2):
            moved[way, 4, n].wait_recv()
        for j in range(n * SJ, (n + 1) * SJ):
            value = part[0, j] + rcv[0, 3, n, j - n * SJ].astype(F32)
            value = value + rcv[1, 3, n, j - n * SJ].astype(F32)
            out[:, j * TILE : (j + 1) * TILE] = value * rec[j]
    for copy in sent:
        copy.wait_send()


def local(
    amplitudes, factors, screening, tile_slot, pair_orbitals, occupied_energy, virtual_energy
):
    arrays = (
        amplitudes, factors, screening.T, tile_slot, pair_orbitals.T, occupied_energy, virtual_energy
    )
    hbm = pl.BlockSpec(memory_space=pltpu.HBM)
    dma = pltpu.SemaphoreType.DMA
    return pl.pallas_call(
        ladder_kernel,
        out_shape=jax.ShapeDtypeStruct((TILE, K * TILE), F32),
        in_specs=[hbm] * 7,
        out_specs=pl.BlockSpec(memory_space=pltpu.VMEM),
        scratch_shapes=[
            pltpu.VMEM((ROWS * TILE, K * TILE), BF16),
            pltpu.VMEM((SLOTS, SL, TILE), BF16),
            pltpu.VMEM((SLOTS, SL, TILE), BF16),
            pltpu.VMEM((SLOTS, SL, TILE), BF16),
            pltpu.VMEM((NQ, NX - 1, K, SL, TILE), BF16),
            pltpu.VMEM((K, TILE, NQ * TILE), BF16),
            pltpu.VMEM((ROWS, K, TILE, NQ * TILE), BF16),
            pltpu.VMEM((2, K, TILE, TILE), F32),
            pltpu.VMEM((2, 4, SUBS, SJ, TILE, TILE), BF16),
            pltpu.VMEM((2, 4, SUBS, SJ, TILE, TILE), BF16),
            pltpu.VMEM((K, TILE, TILE), F32),
            pltpu.SMEM((K, PAIRS), jnp.int32),
            pltpu.SMEM((SLOTS,), jnp.int32),
            pltpu.SMEM((NX, K), jnp.int32),
            pltpu.SMEM((2, PAIRS), jnp.int32),
            pltpu.SMEM((NOCC,), F32),
            pltpu.VMEM((SLOTS, TILE), F32),
            dma,
            dma((5,)),
            dma((NQ,)),
            dma((NQ, NS - 1)),
            dma((NQ, NS - 1)),
            dma((NQ, 4, 2)),
            dma((NQ, 4, 2)),
            dma((NQ, NX - 1)),
            dma((NQ, NX - 1)),
            dma((NQ, NX)),
            dma((NQ, NX)),
            dma((2, 4, SUBS)),
            dma((2, 4, SUBS)),
        ],
        compiler_params=pltpu.CompilerParams(
            collective_id=0, has_side_effects=True, vmem_limit_bytes=48 * 1024 * 1024
        ),
    )(*(pltpu.with_memory_space_constraint(array, pltpu.HBM) for array in arrays))


def solution(mesh):
    return jax.shard_map(
        local,
        mesh=mesh,
        in_specs=(P("pair", None), P("pair", "cuts", None, None), P(), P(), P(), P(), P()),
        out_specs=P(("pair", "cuts"), None),
        check_vma=False,
    )
```

```python
import jax
import jax.numpy as jnp
from jax import lax
from jax.experimental import pallas as pl
from jax.experimental.pallas import tpu as pltpu
from jax.sharding import PartitionSpec as P

TILE = 128
K = 16
NQ = 3
NZ, NX, NC, NY = 8, 4, 2, 8
NS = NX * NC
SL = TILE // NS
SLOTS = 128
PAIRS = 32
NOCC = 4000
BLOCK = SLOTS // NZ
ROWS = 8
SUBS = 4
SJ = K // SUBS
LEAD = NY // 2
BF16 = jnp.bfloat16
F32 = jnp.float32
MESH = pl.DeviceIdType.MESH

SCHEDULE = (
    ("g", 0, 1), ("g", 1, 1), ("g", 2, 1), ("g", 0, 2), ("g", 1, 2), ("g", 0, 3),
    ("g", 2, 2), ("g", 0, 4), ("g", 1, 3), ("g", 2, 3), ("d", 0, 0), ("g", 1, 4),
    ("g", 2, 4), ("d", 1, 0), ("e", 0, 0), ("d", 2, 0),
)


def ladder_kernel(
    amp, fac, screen_in, slot_in, orb_in, occ_in, virt_in, out,
    a_buf, gath0, gath1, gath2, sel, tiles, half, part, snd, rcv, rec,
    screen, slot_of, wanted, orb, occ, virt, a_sem, in_sem, loc_sem, sp_s, sp_r, ag_s, ag_r, dl_s, dl_r, ex_s, ex_r, rs_s, rs_r,
):
    gath = (gath0, gath1, gath2)
    pair = lax.axis_index("pair")
    y = lax.axis_index("cuts")
    s = lax.rem(pair, NS)
    z = pair // NS
    x = s // NC
    core = lax.rem(s, NC)
    p = pair // NC

    def wrap(value, n):
        return lax.rem(value + n, n)

    z_up, z_down = wrap(z + 1, NZ) * NS + s, wrap(z - 1, NZ) * NS + s
    y_up, y_down = wrap(y + 1, NY), wrap(y - 1, NY)

    load_a = pltpu.make_async_copy(amp, a_buf, a_sem)
    load_a.start()
    loads = [
        pltpu.make_async_copy(src, dst, in_sem.at[n])
        for n, (src, dst) in enumerate(
            ((screen_in, screen), (slot_in, slot_of), (orb_in, orb), (occ_in, occ), (virt_in, virt))
        )
    ]
    for load in loads:
        load.start()

    barrier = pltpu.get_barrier_semaphore()
    peers = [(z * NS + wrap(s + d, NS), y) for d in range(1, NS)]
    peers += [(z_up, y), (z_down, y), (pair, y_up), (pair, y_down)]
    for peer in peers:
        pl.semaphore_signal(barrier, inc=1, device_id=peer, device_id_type=MESH)
    pl.semaphore_wait(barrier, len(peers))

    def remote(src, dst, send, recv, device):
        copy = pltpu.make_async_remote_copy(
            src_ref=src, dst_ref=dst, send_sem=send, recv_sem=recv,
            device_id=device, device_id_type=MESH,
        )
        copy.start()
        return copy

    sent = []

    spread = {}
    mine = pl.ds(z * BLOCK + s * 2, 2)
    for q in range(NQ):
        rows = pl.ds(pl.multiple_of(s * SL, SL), SL)
        own = pltpu.make_async_copy(fac.at[:, q, rows, :], gath[q].at[mine], loc_sem.at[q])
        own.start()
        spread[q] = [own]
        for d in (4, 3, 5, 2, 6, 1, 7):
            to = wrap(s + d, NS)
            rows = pl.ds(pl.multiple_of(to * SL, SL), SL)
            spread[q].append(
                remote(
                    fac.at[:, q, rows, :], gath[q].at[mine],
                    sp_s.at[q, d - 1], sp_r.at[q, d - 1], (z * NS + to, y),
                )
            )
        sent += spread[q][1:]

    def look_up():
        for load in loads:
            load.wait()
        for dx in range(NX):
            its_pair = z * NX + wrap(x + dx, NX)

            def want(k, _):
                wanted[dx, k] = slot_of[screen[k, its_pair]]
                return 0

            lax.fori_loop(0, K, want, 0, unroll=4)

    def denominators():
        first = occ[orb[0, p]]
        second = occ[orb[1, p]]
        row = virt[pl.ds(screen[core * ROWS + y, p], 1), :] - first
        row = jnp.transpose(jnp.broadcast_to(row, (TILE, TILE)))

        def denominator(j, _):
            col = virt[pl.ds(screen[j, p], 1), :] - second
            rec[j] = 1.0 / (row + col)
            return 0

        lax.fori_loop(0, K, denominator, 0)

    ring = {}

    def gather_step(q, t):
        if t == 1:
            spread[q][0].wait()
            for copy in spread[q][1:]:
                copy.wait_recv()
        for way in range(2):
            if t > 1:
                ring[q, t - 1, way].wait_recv()
            if way == 0:
                start, to = wrap(z - (t - 1), NZ) * BLOCK, z_up
            else:
                start, to = wrap(z + (t - 1), NZ) * BLOCK, z_down
            count = BLOCK
            if t == NZ // 2:
                count = BLOCK // 2
                start = start + way * count
            block = gath[q].at[pl.ds(start, count)]
            ring[q, t, way] = remote(
                block, block, ag_s.at[q, t - 1, way], ag_r.at[q, t - 1, way], (to, y)
            )
            sent.append(ring[q, t, way])

    delivered = {}

    def deliver(q):
        for way in range(2):
            ring[q, NZ // 2, way].wait_recv()
        lanes = pl.ds(q * TILE, TILE)
        rows = pl.ds(pl.multiple_of(s * SL, SL), SL)
        for dx in (2, 1, 3, 0):
            to = wrap(x + dx, NX)
            for k in range(K):
                value = gath[q][wanted[dx, k]]
                if dx == 0:
                    tiles[k, rows, lanes] = value
                else:
                    sel[q, dx - 1, k] = value
            if dx:
                delivered[q, dx] = remote(
                    sel.at[q, dx - 1], tiles.at[:, rows, lanes],
                    dl_s.at[q, dx - 1], dl_r.at[q, dx - 1], (z * NS + to * NC + core, y),
                )
                sent.append(delivered[q, dx])

    exchanged = {}

    def exchange(q):
        lanes = pl.ds(q * TILE, TILE)
        for dx in (0, 1, 3, 2):
            if dx:
                delivered[q, dx].wait_recv()
            rows = pl.ds(pl.multiple_of((wrap(x - dx, NX) * NC + core) * SL, SL), SL)
            block = tiles.at[:, rows, lanes]
            exchanged[q, dx] = remote(
                block, block, ex_s.at[q, dx], ex_r.at[q, dx], (z * NS + x * NC + 1 - core, y)
            )
            sent.append(exchanged[q, dx])

    def first_product(q, start=0, count=ROWS):
        if start == 0:
            for dx in range(NX):
                exchanged[q, dx].wait_recv()
        lanes = pl.ds(q * TILE, TILE)

        def one_row(n, _):
            i = wrap(y + LEAD + n, ROWS)
            left = tiles[core * ROWS + i, :, lanes]
            rows = pl.ds(pl.multiple_of(i * TILE, TILE), TILE)
            for c in range(4):
                value = jnp.dot(
                    left, a_buf[rows, c * 512 : (c + 1) * 512], preferred_element_type=F32
                ).astype(BF16)
                for jj in range(4):
                    half[i, c * 4 + jj, :, lanes] = value[:, jj * TILE : (jj + 1) * TILE]
            return 0

        lax.fori_loop(start, start + count, one_row, 0)

    for step in SCHEDULE:
        if step[0] == "g":
            gather_step(step[1], step[2])
        elif step[0] == "d":
            deliver(step[1])
        else:
            exchange(step[1])
        if step == ("g", 2, 1):
            look_up()
    load_a.wait()
    exchange(1)
    first_product(0)
    exchange(2)
    first_product(1)
    first_product(2, 0, 1)

    def partial(r, slot, start=0, count=K):
        def one_column(j, _):
            part[slot, j] = lax.dot_general(
                half[r, j], tiles[j], (((1,), (1,)), ((), ())), preferred_element_type=F32
            )
            return 0

        lax.fori_loop(start, start + count, one_column, 0, unroll=min(count, 8))

    moved = {}

    def send(way, t, sub, slot, add):
        value = part[slot, sub * SJ : (sub + 1) * SJ]
        if add:
            moved[way, t - 1, sub].wait_recv()
            value = value + rcv[way, t - 2, sub].astype(F32)
        snd[way, t - 1, sub] = value.astype(BF16)
        moved[way, t, sub] = remote(
            snd.at[way, t - 1, sub], rcv.at[way, t - 1, sub],
            rs_s.at[way, t - 1, sub], rs_r.at[way, t - 1, sub],
            (pair, y_up if way == 0 else y_down),
        )
        sent.append(moved[way, t, sub])

    long_subs = ((0, 1), (2, 3))
    short_subs = ((2, 3), (0, 1))
    for n in range(2):
        for way in range(2):
            sub = long_subs[way][n]
            partial(wrap(y + LEAD, NY), 0, sub * SJ, SJ)
            send(way, 1, sub, 0, False)
    first_product(2, 1, ROWS - 1)
    denominators()
    for t in range(2, 5):
        partial(wrap(y + 5 - t, NY), 0)
        partial(wrap(y - 5 + t, NY), 1)
        for n in range(2):
            for way in range(2):
                send(way, t, short_subs[way][n], way, t > 2)
        for n in range(2):
            for way in range(2):
                send(way, t, long_subs[way][n], way, True)
    partial(y, 0)
    for n in (2, 0, 3, 1):
        for way in range(2):
            moved[way, 4, n].wait_recv()
        for j in range(n * SJ, (n + 1) * SJ):
            value = part[0, j] + rcv[0, 3, n, j - n * SJ].astype(F32)
            value = value + rcv[1, 3, n, j - n * SJ].astype(F32)
            out[:, j * TILE : (j + 1) * TILE] = value * rec[j]
    for copy in sent:
        copy.wait_send()


def local(
    amplitudes, factors, screening, tile_slot, pair_orbitals, occupied_energy, virtual_energy
):
    arrays = (
        amplitudes, factors, screening.T, tile_slot, pair_orbitals.T, occupied_energy, virtual_energy
    )
    hbm = pl.BlockSpec(memory_space=pltpu.HBM)
    dma = pltpu.SemaphoreType.DMA
    return pl.pallas_call(
        ladder_kernel,
        out_shape=jax.ShapeDtypeStruct((TILE, K * TILE), F32),
        in_specs=[hbm] * 7,
        out_specs=pl.BlockSpec(memory_space=pltpu.VMEM),
        scratch_shapes=[
            pltpu.VMEM((ROWS * TILE, K * TILE), BF16),
            pltpu.VMEM((SLOTS, SL, TILE), BF16),
            pltpu.VMEM((SLOTS, SL, TILE), BF16),
            pltpu.VMEM((SLOTS, SL, TILE), BF16),
            pltpu.VMEM((NQ, NX - 1, K, SL, TILE), BF16),
            pltpu.VMEM((K, TILE, NQ * TILE), BF16),
            pltpu.VMEM((ROWS, K, TILE, NQ * TILE), BF16),
            pltpu.VMEM((2, K, TILE, TILE), F32),
            pltpu.VMEM((2, 4, SUBS, SJ, TILE, TILE), BF16),
            pltpu.VMEM((2, 4, SUBS, SJ, TILE, TILE), BF16),
            pltpu.VMEM((K, TILE, TILE), F32),
            pltpu.SMEM((K, PAIRS), jnp.int32),
            pltpu.SMEM((SLOTS,), jnp.int32),
            pltpu.SMEM((NX, K), jnp.int32),
            pltpu.SMEM((2, PAIRS), jnp.int32),
            pltpu.SMEM((NOCC,), F32),
            pltpu.VMEM((SLOTS, TILE), F32),
            dma,
            dma((5,)),
            dma((NQ,)),
            dma((NQ, NS - 1)),
            dma((NQ, NS - 1)),
            dma((NQ, 4, 2)),
            dma((NQ, 4, 2)),
            dma((NQ, NX - 1)),
            dma((NQ, NX - 1)),
            dma((NQ, NX)),
            dma((NQ, NX)),
            dma((2, 4, SUBS)),
            dma((2, 4, SUBS)),
        ],
        compiler_params=pltpu.CompilerParams(
            collective_id=0, has_side_effects=True, vmem_limit_bytes=48 * 1024 * 1024
        ),
    )(*(pltpu.with_memory_space_constraint(array, pltpu.HBM) for array in arrays))


def solution(mesh):
    return jax.shard_map(
        local,
        mesh=mesh,
        in_specs=(P("pair", None), P("pair", "cuts", None, None), P(), P(), P(), P(), P()),
        out_specs=P(("pair", "cuts"), None),
        check_vma=False,
    )
```
